512 devices in a mesh: tm: 16 (over y, z_hi), height: 8 (over x, core), head: 4 (over z_lo).
Axes of the slice: x: 4, y: 4, z: 16 (z_hi: 4, z_lo: 4; z = z_hi * 4 + z_lo), core: 2. Of those that a mesh axis runs over, the one named last changes fastest.
Arguments:
- queries: bfloat16 [16, 8, 128, 3072], P('tm', 'height', None, 'head'), may hold values from -8 to 8
- keys: bfloat16 [16, 8, 128, 3072], P('tm', 'height', None, 'head'), may hold values from -8 to 8
- values: bfloat16 [16, 8, 128, 3072], P('tm', 'height', None, 'head'), may hold values from -6 to 6
- grad_out: bfloat16 [16, 8, 128, 3072], P('tm', 'height', None, 'head'), may hold values from -6 to 6
- caption_keys: bfloat16 [256, 3072], P(None, 'head'), may hold values from -6 to 6
- caption_values: bfloat16 [256, 3072], P(None, 'head'), may hold values from -6 to 6
- caption_mask: int32 [256], replicated, may hold values 0 or 1
- kept: int32 [16, 8, 4], P('tm', 'height'), may hold values 0 or 1
Outputs:
- attended: bfloat16 [16, 8, 128, 3072], P('tm', 'height', None, 'head')
- query_grad: bfloat16 [16, 8, 128, 3072], P('tm', 'height', None, 'head')
- key_grad: bfloat16 [16, 8, 128, 3072], P('tm', 'height', None, 'head')
- value_grad: bfloat16 [16, 8, 128, 3072], P('tm', 'height', None, 'head')
- caption_key_grad: bfloat16 [256, 3072], P(None, 'head')
- caption_value_grad: bfloat16 [256, 3072], P(None, 'head')
The draws below stay inside these ranges and needn't reach their ends.
All inputs are finite; a program needn't handle non-finite values. No bound on the sum of `kept` on one device may be relied on, other than what follows from the above.
Results may differ from the reference program's by a relative error of at most 0.029.
Values may be sent and summed in bfloat16 or wider, within the bound.
No kernel may reach another device: no remote copies, remote signals or barrier semaphores. Data moves between devices by JAX's collectives and lax.ppermute only.
A program may use at most 64 MiB of HBM per device.

```python
import math
import jax
import jax.numpy as jnp
from jax import lax

D = 3072
HEADS = 24
HD = 128
TILE = 128
CAP = 256
NT = 16
NH = 8


def base_draw(key):
    return jnp.clip(jax.random.normal(key, (NT, NH, TILE, D), jnp.float32), -6.0, 6.0)


def draw_queries(key, part):
    result = base_draw(jax.random.fold_in(key, 21))
    return result.astype(jnp.bfloat16)


def draw_keys(key, part):
    result = base_draw(jax.random.fold_in(key, 22))
    return result.astype(jnp.bfloat16)


def with_ends(drawn, stream_key, least, top_value):
    place = [jax.random.randint(jax.random.fold_in(stream_key, axis), (), 0, length) for axis, length in enumerate(drawn.shape)]
    widest = drawn.shape.index(max(drawn.shape))
    next_to = place[:widest] + [(place[widest] + 1) % drawn.shape[widest]] + place[widest + 1:]
    return drawn.at[tuple(place)].set(least).at[tuple(next_to)].set(top_value)


def steps_of(stream_key, shape, pieces, least, high):
    factor_of, own = 1.0, jax.random.fold_in(stream_key, 6)
    for axis_at, shards_of in pieces:
        draws = jnp.exp(jax.random.uniform(jax.random.fold_in(own, axis_at), (shards_of,), jnp.float32, least / len(pieces), high / len(pieces)))
        factor_of = factor_of * jnp.repeat(draws, shape[axis_at] // shards_of).reshape([-1 if axis == axis_at else 1 for axis in range(len(shape))])
    return factor_of


def bell_draw(key, extent, spread, limit, shards=(), kind=jnp.bfloat16):
    gain = steps_of(key, extent, shards, -0.22, 0.18) if shards else 1.0
    values = jax.random.normal(key, extent, jnp.float32) * spread * gain
    return jnp.minimum(jnp.maximum(values, -limit), limit).astype(kind)


def setup_inputs(seed: int = 0) -> dict:
    seeds = jax.random.split(jax.random.key(seed), 9)
    queries = draw_queries(jax.random.fold_in(seeds[8], 71), 0)
    keys = draw_keys(jax.random.fold_in(seeds[8], 71), 0)
    values = bell_draw(seeds[2], (NT, NH, TILE, D), 1.0, 6.0, ((0, 16), (1, 8), (3, 4)))
    grad_out = bell_draw(seeds[3], (NT, NH, TILE, D), 1.0, 6.0, ((0, 16), (1, 8), (3, 4)))
    caption_keys = bell_draw(seeds[4], (CAP, D), 1.0, 6.0, ((1, 4),))
    caption_values = bell_draw(seeds[5], (CAP, D), 1.0, 6.0, ((1, 4),))
    caption_mask = with_ends((jax.random.randint(seeds[6], (CAP,), 0, 4) < 3).astype(jnp.int32), jax.random.fold_in(seeds[6], 1), 0, 1)
    kept = with_ends((jax.random.randint(seeds[7], (NT, NH, 4), 0, 2) < 1).astype(jnp.int32), jax.random.fold_in(seeds[7], 1), 0, 1)
    return {"queries": queries, "keys": keys, "values": values, "grad_out": grad_out, "caption_keys": caption_keys, "caption_values": caption_values, "caption_mask": caption_mask, "kept": kept}


def split_heads(array):
    return array.reshape(array.shape[:-1] + (HEADS, HD)).astype(jnp.float32)

def round_half(array):
    return lax.optimization_barrier(array.astype(jnp.bfloat16)).astype(jnp.float32)

def padded(array):
    return jnp.pad(array, ((1, 1), (1, 1)) + ((0, 0),) * (array.ndim - 2))

def reference(queries, keys, values, grad_out, caption_keys, caption_values, caption_mask, kept):
    score_scale = 1.0 / math.sqrt(HD)
    time_grid = jnp.arange(NT, dtype=jnp.int32)[:, None] + jnp.zeros((1, NH), jnp.int32)
    band_grid = jnp.arange(NH, dtype=jnp.int32)[None, :] + jnp.zeros((NT, 1), jnp.int32)
    inside = jnp.stack([time_grid > 0, time_grid < NT - 1, band_grid > 0, band_grid < NH - 1], axis=-1)
    linked = (kept > 0) & inside
    padded_keys = padded(keys)
    padded_values = padded(values)
    caption_key_heads = split_heads(caption_keys)
    caption_value_heads = split_heads(caption_values)
    caption_usable = caption_mask > 0
    offsets = ((1, 1), (0, 1), (2, 1), (1, 0), (1, 2))

    def forward_tile(totals, tile_index):
        time_at = tile_index // NH
        band_at = tile_index % NH
        key_rows = jnp.concatenate([padded_keys[time_at + slot_time, band_at + slot_band] for slot_time, slot_band in offsets], axis=0)
        value_rows = jnp.concatenate([padded_values[time_at + slot_time, band_at + slot_band] for slot_time, slot_band in offsets], axis=0)
        key_heads = jnp.concatenate([split_heads(key_rows), caption_key_heads], axis=0)
        value_heads = jnp.concatenate([split_heads(value_rows), caption_value_heads], axis=0)
        usable = jnp.concatenate([jnp.ones((TILE,), jnp.bool_)] + [jnp.full((TILE,), linked[time_at, band_at, direction]) for direction in range(4)] + [caption_usable])
        query_heads = split_heads(queries[time_at, band_at])
        cotangent = split_heads(grad_out[time_at, band_at])
        scores = jnp.einsum('rhd,khd->hrk', query_heads, key_heads) * score_scale
        scores = jnp.where(usable, scores, -jnp.inf)
        row_top = lax.optimization_barrier(jnp.max(scores, axis=-1, keepdims=True))
        log_total = row_top + jnp.log(lax.optimization_barrier(jnp.sum(jnp.exp(scores - row_top), axis=-1, keepdims=True)))
        weights = jnp.exp(scores - log_total)
        weights_half = round_half(weights)
        out_tile = jnp.einsum('hrk,khd->rhd', weights_half, value_heads).reshape(TILE, D).astype(jnp.bfloat16)
        row_delta = lax.optimization_barrier(jnp.sum(split_heads(out_tile) * cotangent, axis=-1)).T[:, :, None]
        dweights = jnp.einsum('rhd,khd->hrk', cotangent, value_heads)
        dscores = round_half(weights * (dweights - row_delta))
        dquery = (jnp.einsum('hrk,khd->rhd', dscores, key_heads) * score_scale).reshape(TILE, D).astype(jnp.bfloat16)
        caption_dk = jnp.einsum('hrk,rhd->khd', dscores[:, :, 5 * TILE:], query_heads) * score_scale
        caption_dv = jnp.einsum('hrk,rhd->khd', weights_half[:, :, 5 * TILE:], cotangent)
        totals = (totals[0] + caption_dk.reshape(CAP, D), totals[1] + caption_dv.reshape(CAP, D))
        return (totals, (out_tile, dquery, log_total[:, :, 0], row_delta[:, :, 0]))
    start_totals = (jnp.zeros((CAP, D), jnp.float32), jnp.zeros((CAP, D), jnp.float32))
    tile_numbers = jnp.arange(NT * NH, dtype=jnp.int32)
    caption_sums, per_tile = lax.scan(forward_tile, start_totals, tile_numbers)
    attended = per_tile[0].reshape(NT, NH, TILE, D)
    query_grad = per_tile[1].reshape(NT, NH, TILE, D)
    log_totals = per_tile[2].reshape(NT, NH, HEADS, TILE)
    row_deltas = per_tile[3].reshape(NT, NH, HEADS, TILE)
    padded_queries = padded(queries)
    padded_grads = padded(grad_out)
    padded_totals = padded(log_totals)
    padded_deltas = padded(row_deltas)
    padded_links = padded(linked)
    sources = ((2, 1, 0), (0, 1, 1), (1, 2, 2), (1, 0, 3))

    def key_tile(tile_index):
        time_at = tile_index // NH
        band_at = tile_index % NH
        key_heads = split_heads(keys[time_at, band_at])
        value_heads = split_heads(values[time_at, band_at])
        query_stack = jnp.stack([queries[time_at, band_at]] + [padded_queries[time_at + slot_time, band_at + slot_band] for slot_time, slot_band, direction in sources])
        grad_stack = jnp.stack([grad_out[time_at, band_at]] + [padded_grads[time_at + slot_time, band_at + slot_band] for slot_time, slot_band, direction in sources])
        total_stack = jnp.stack([log_totals[time_at, band_at]] + [padded_totals[time_at + slot_time, band_at + slot_band] for slot_time, slot_band, direction in sources])
        delta_stack = jnp.stack([row_deltas[time_at, band_at]] + [padded_deltas[time_at + slot_time, band_at + slot_band] for slot_time, slot_band, direction in sources])
        usable = jnp.stack([jnp.array(True)] + [padded_links[time_at + slot_time, band_at + slot_band, direction] for slot_time, slot_band, direction in sources])
        query_heads = split_heads(query_stack)
        cotangent = split_heads(grad_stack)
        scores = jnp.einsum('nrhd,khd->nhrk', query_heads, key_heads) * score_scale
        weights = jnp.where(usable[:, None, None, None], jnp.exp(scores - total_stack[..., None]), 0.0)
        weights_half = round_half(weights)
        dweights = jnp.einsum('nrhd,khd->nhrk', cotangent, value_heads)
        dscores = round_half(weights * (dweights - delta_stack[..., None]))
        dkey = jnp.einsum('nhrk,nrhd->khd', dscores, query_heads) * score_scale
        dvalue = jnp.einsum('nhrk,nrhd->khd', weights_half, cotangent)
        return (dkey.reshape(TILE, D).astype(jnp.bfloat16), dvalue.reshape(TILE, D).astype(jnp.bfloat16))
    key_grad, value_grad = lax.map(key_tile, tile_numbers)
    key_grad = key_grad.reshape(NT, NH, TILE, D)
    value_grad = value_grad.reshape(NT, NH, TILE, D)
    return (attended, query_grad, key_grad, value_grad, caption_sums[0].astype(jnp.bfloat16), caption_sums[1].astype(jnp.bfloat16))
```

```python
import math

import jax
import jax.numpy as jnp
from jax import lax
from jax.experimental import pallas as pl
from jax.experimental.pallas import tpu as pltpu
from jax.sharding import Mesh
from jax.sharding import PartitionSpec as P

HD = 128
TILE = 128
NEG = -1e30
NY, NZ, NB = 4, 4, 8
BF = jnp.bfloat16
F32 = jnp.float32


def attend_kernel(
    link_ref, mask_ref, q_ref, k_ref, v_ref, g_ref,
    k0, v0, k1, v1, k2, v2, k3, v3, ck_ref, cv_ref,
    out_ref, dq_ref, own_ref, n0, n1, n2, n3, cap_ref,
):
    scale = 1.0 / math.sqrt(HD)
    q = q_ref[...]
    g = g_ref[...]
    key = jnp.concatenate([k_ref[...], k0[...], k1[...], k2[...], k3[...], ck_ref[...]], axis=0)
    val = jnp.concatenate([v_ref[...], v0[...], v1[...], v2[...], v3[...], cv_ref[...]], axis=0)
    nt = (((1,), (1,)), ((), ()))
    nn = (((1,), (0,)), ((), ()))
    tn = (((0,), (0,)), ((), ()))
    dot = lambda a, b, dims: lax.dot_general(a, b, dims, preferred_element_type=F32)
    usable = jnp.concatenate(
        [jnp.ones((1, TILE), jnp.int32)]
        + [jnp.full((1, TILE), link_ref[d], jnp.int32) for d in range(4)]
        + [mask_ref[...]],
        axis=1,
    )
    scores = dot(q, key, nt) * scale
    scores = jnp.where(usable > 0, scores, NEG)
    top = jnp.max(scores, axis=-1, keepdims=True)
    expo = jnp.exp(scores - top)
    weights = expo * (1.0 / jnp.sum(expo, axis=-1, keepdims=True))
    wb = weights.astype(BF)
    out = dot(wb, val, nn).astype(BF)
    out_ref[...] = out
    delta = jnp.sum(out.astype(F32) * g.astype(F32), axis=-1, keepdims=True)
    dw = dot(g, val, nt)
    ds = (weights * (dw - delta)).astype(BF)
    dq_ref[...] = (dot(ds, key, nn) * scale).astype(BF)
    dk = dot(ds, q, tn) * scale
    dv = dot(wb, g, tn)
    own_ref[0] = dk[:TILE]
    own_ref[1] = dv[:TILE]
    for d, ref in enumerate((n0, n1, n2, n3)):
        rows = slice((d + 1) * TILE, (d + 2) * TILE)
        ref[0] = dk[rows].astype(BF)
        ref[1] = dv[rows].astype(BF)
    cap = cap_ref.shape[0] // 2
    cap_ref[:cap] = dk[5 * TILE :].astype(BF)
    cap_ref[cap:] = dv[5 * TILE :].astype(BF)


def attend(link, mask, q, k, v, g, near, ck, cv):
    width = q.shape[1]
    heads = width // HD
    cap = ck.shape[0]
    tile = pl.BlockSpec((TILE, HD), lambda h: (0, h))
    caption = pl.BlockSpec((cap, HD), lambda h: (0, h))
    pair = pl.BlockSpec((2, TILE, HD), lambda h: (0, 0, h))
    pair_b = jax.ShapeDtypeStruct((2, TILE, width), BF)
    return pl.pallas_call(
        attend_kernel,
        grid=(heads,),
        in_specs=[
            pl.BlockSpec(memory_space=pltpu.SMEM),
            pl.BlockSpec((1, cap), lambda h: (0, 0)),
        ]
        + [tile] * 12
        + [caption] * 2,
        out_specs=[tile, tile, pair, pair, pair, pair, pair, pl.BlockSpec((2 * cap, HD), lambda h: (0, h))],
        out_shape=[
            jax.ShapeDtypeStruct((TILE, width), BF),
            jax.ShapeDtypeStruct((TILE, width), BF),
            jax.ShapeDtypeStruct((2, TILE, width), F32),
            pair_b,
            pair_b,
            pair_b,
            pair_b,
            jax.ShapeDtypeStruct((2 * cap, width), BF),
        ],
    )(link, mask, q, k, v, g, *near, ck, cv)


def shift(array, axes, count, by):
    pairs = [(i, i + by) for i in range(count) if 0 <= i + by < count]
    return lax.ppermute(array, axes, pairs)


def sum_kernel(got_ref, sum_ref):
    total = jnp.sum(got_ref[...].astype(F32), axis=0).astype(BF)
    sum_ref[...] = jnp.broadcast_to(total, sum_ref.shape)


def sum_and_copy(got, copies):
    return pl.pallas_call(
        sum_kernel,
        out_shape=jax.ShapeDtypeStruct((copies,) + got.shape[1:], BF),
    )(got)


def reduce_captions(part):
    rows, width = part.shape
    plane = ("ty", "height")
    members = NY * NB
    got = lax.all_to_all(part.reshape(members, rows // members, width), plane, 0, 0, tiled=True)
    got = lax.all_to_all(sum_and_copy(got, NZ), "tz", 0, 0, tiled=True)
    got = lax.all_to_all(sum_and_copy(got, members), plane, 0, 0, tiled=True)
    return got.reshape(rows, width)


def body(queries, keys, values, grad_out, caption_keys, caption_values, caption_mask, kept):
    tm = ("ty", "tz")
    shape = queries.shape
    q, k, v, g = (a[0, 0] for a in (queries, keys, values, grad_out))
    count_t = NY * NZ
    near = []
    for axes, count in ((tm, count_t), ("height", NB)):
        for by in (1, -1):
            near += [shift(k, axes, count, by), shift(v, axes, count, by)]
    time_pos = lax.axis_index("ty") * NZ + lax.axis_index("tz")
    band_pos = lax.axis_index("height")
    inside = jnp.stack([time_pos > 0, time_pos < count_t - 1, band_pos > 0, band_pos < NB - 1])
    link = ((kept[0, 0] > 0) & inside).astype(jnp.int32)
    mask = (caption_mask > 0).astype(jnp.int32)[None]
    out, dq, own, n0, n1, n2, n3, cap = attend(
        link, mask, q, k, v, g, near, caption_keys, caption_values
    )
    arrived = [
        shift(n0, tm, count_t, -1),
        shift(n1, tm, count_t, 1),
        shift(n2, "height", NB, -1),
        shift(n3, "height", NB, 1),
    ]
    captions = reduce_captions(cap)
    total = own
    for piece in arrived:
        total = total + piece.astype(F32)
    total = total.astype(BF)
    tokens = caption_keys.shape[0]
    return (
        out.reshape(shape),
        dq.reshape(shape),
        total[0].reshape(shape),
        total[1].reshape(shape),
        captions[:tokens],
        captions[tokens:],
    )


def solution(mesh):
    devices = mesh.devices
    split = Mesh(
        devices.reshape((NY, NZ) + devices.shape[1:]), ("ty", "tz", "height", "head")
    )
    tile = P(("ty", "tz"), "height", None, "head")
    caption = P(None, "head")
    return jax.shard_map(
        body,
        mesh=split,
        in_specs=(tile,) * 4 + (caption, caption, P(), P(("ty", "tz"), "height", None)),
        out_specs=(tile,) * 4 + (caption, caption),
        check_vma=False,
    )
```
